512 devices in a mesh: context: 32 (over x, y, z_hi), tensor: 16 (over z_lo, core).
Axes of the slice: x: 4, y: 4, z: 16 (z_hi: 2, z_lo: 8; z = z_hi * 8 + z_lo), core: 2. Of those that a mesh axis runs over, the one named last changes fastest.
Arguments:
- inputs: float32 [128, 131072], P('tensor', 'context'), may hold values from -0.0390625 to 0.0390625
- grads: float32 [128, 131072], P('tensor', 'context'), may hold values from -6 to 6
- response: float32 [128, 131072], P('tensor', 'context'), may hold values from -0.0390625 to 0.0390625
Outputs:
- input_grad: float32 [128, 131072], P('tensor', 'context')
- filter_grad: float32 [128, 131072], P('tensor', 'context')
The draws below stay inside these ranges and needn't reach their ends.
All inputs are finite; a program needn't handle non-finite values.
Results may differ from the reference program's by a relative error of at most 0.00014.
Values sent between devices are 32-bit elements; how exact they have to be, the bound alone decides.
A program may use at most 64 MiB of HBM per device.

```python
import jax
import jax.numpy as jnp
from jax import lax

CH_DEV = 8
CH = 128
LEN = 131072
N_TENSOR = 16


def level_of(rng, dims, shards, least, largest):
    level = 1.0
    for dim, shards_of in shards:
        draws = jax.random.uniform(jax.random.fold_in(jax.random.fold_in(rng, 6), dim), (shards_of,), jnp.float32, least / len(shards), largest / len(shards))
        level = level * jnp.repeat(jnp.exp(draws), dims[dim] // shards_of).reshape((-1,) + (1,) * (len(dims) - 1 - dim))
    return level


def scatter_about(key, dims, scale, reach, cuts=(), kind=jnp.bfloat16):
    drawn = scale * jax.random.normal(key, dims, jnp.float32)
    if cuts:
        drawn = drawn * level_of(key, dims, cuts, -0.22, 0.18)
    return jnp.clip(drawn, -reach, reach).astype(kind)


def setup_inputs(seed: int = 0) -> dict:
    splits = jax.random.split(jax.random.key(seed), 4)
    inputs = scatter_about(splits[0], (CH, LEN), (LEN ** -0.5), 0.0390625, ((0, 16), (1, 32)), jnp.float32)
    grads = scatter_about(splits[1], (CH, LEN), 1.0, 6.0, ((0, 16), (1, 32)), jnp.float32)
    response = scatter_about(splits[2], (CH, LEN), (LEN ** -0.5), 0.0390625, ((0, 16), (1, 32)), jnp.float32)
    return {"inputs": inputs, "grads": grads, "response": response}


def channel_group(packed):
    signal_in, signal_grad, signal_filter = packed
    padded_len = 2 * LEN
    input_spec = jnp.fft.fft(signal_in, n=padded_len)
    grad_spec = jnp.fft.fft(signal_grad, n=padded_len)
    filter_spec = jnp.fft.fft(signal_filter, n=padded_len)
    input_grad = jnp.real(jnp.fft.ifft(jnp.conj(filter_spec) * grad_spec))[:, :LEN]
    filter_grad = jnp.real(jnp.fft.ifft(jnp.conj(input_spec) * grad_spec))[:, :LEN]
    return input_grad, filter_grad


def reference(inputs, grads, response):
    shaped_in = inputs.reshape(N_TENSOR, CH_DEV, LEN)
    shaped_grad = grads.reshape(N_TENSOR, CH_DEV, LEN)
    shaped_filter = response.reshape(N_TENSOR, CH_DEV, LEN)
    input_grad, filter_grad = lax.map(channel_group, (shaped_in, shaped_grad, shaped_filter))
    return input_grad.reshape(CH_DEV * N_TENSOR, LEN), filter_grad.reshape(CH_DEV * N_TENSOR, LEN)
```

```python
import functools

import jax
import jax.numpy as jnp
import numpy as np
from jax import lax
from jax.experimental import pallas as pl
from jax.experimental.pallas import tpu as pltpu
from jax.sharding import PartitionSpec as P

PLANE = 16
HALF = 4
GROUP = 8
A, B = 64, 128
BLOCK = A * B


def split_bf16(table):
    high = table.astype(jnp.bfloat16)
    low = (table - high.astype(np.float64)).astype(jnp.bfloat16)
    return high, low


def tables():
    a, b = np.arange(A), np.arange(B)
    first = 2 * np.pi * (np.arange(A)[:, None] + 0.25) * a[None, :] / A
    last = 2 * np.pi * (np.arange(B)[:, None] * b[None, :] % B) / B
    twist = -2 * np.pi * (np.arange(A)[:, None] + 0.25) * b[None, :] / BLOCK
    fwd1 = np.concatenate([np.cos(first), -np.sin(first)], 0)
    fwd2 = np.block([[np.cos(last), -np.sin(last)], [np.sin(last), np.cos(last)]])
    inv1 = np.block([[np.cos(last), np.sin(last)], [-np.sin(last), np.cos(last)]])
    inv2 = np.concatenate([np.cos(first).T, -np.sin(first).T], 1) / BLOCK
    h, l = split_bf16(fwd1)
    fwd1 = np.concatenate([h, l, h], 1)
    h, l = split_bf16(fwd2)
    fwd2 = np.concatenate([h, l, h], 0)
    h, l = split_bf16(inv1)
    inv1 = np.concatenate([h, l, h], 0)
    h, l = split_bf16(inv2)
    inv2 = np.concatenate([h, l, h], 1)
    turn = np.stack([np.cos(twist), np.sin(twist)]).astype(np.float32)
    return fwd1, fwd2, inv1, inv2, turn


def tripled(value, axis):
    high = value.astype(jnp.bfloat16)
    low = (value - high.astype(jnp.float32)).astype(jnp.bfloat16)
    return jnp.concatenate([high, high, low], axis=axis)


def mm(left, right):
    return jnp.dot(left, right, preferred_element_type=jnp.float32)


def kernel(
    x_hbm, g_hbm, r_hbm, fwd1_hbm, fwd2_hbm, inv1_hbm, inv2_hbm, turn_hbm,
    dx_ref, dr_ref,
    raw, rows, mine, vin, fsend, frecv, bsend, brecv, yout, yrecv, orow,
    fwd1, fwd2, inv1, inv2, turn,
    in_sem, z1s, z1r, fs, fr, bs, br, z2s, z2r,
):
    ctx = lax.axis_index("context")
    h = lax.rem(ctx, 2)
    m = lax.div(ctx, 2)
    gx, gy = lax.div(m, 4), lax.rem(m, 4)
    group = lax.rem(gx + gy, 2)
    place = 2 * gx + lax.div(gy, 2)
    partner = {"context": 2 * m + 1 - h}

    barrier = pltpu.get_barrier_semaphore()
    pl.semaphore_signal(barrier, 1, device_id=partner)
    for i in range(1, PLANE):
        pl.semaphore_signal(barrier, 1, device_id={"context": 2 * lax.rem(m + i, PLANE) + h})

    loads = [
        pltpu.make_async_copy(src, dst, in_sem.at[i])
        for i, (src, dst) in enumerate(
            [(x_hbm, raw.at[0]), (g_hbm, raw.at[1]), (r_hbm, raw.at[2]),
             (fwd1_hbm, fwd1), (fwd2_hbm, fwd2), (inv1_hbm, inv1), (inv2_hbm, inv2), (turn_hbm, turn)]
        )
    ]
    for copy in loads:
        copy.start()
    for copy in loads[:3]:
        copy.wait()
    for s in range(3):
        for a in range(32):
            rows[s, 8 * a : 8 * a + 8, :] = raw[s, :, 128 * a : 128 * a + 128]
    for s in range(3):
        for ch in range(8):
            mine[ch, s] = rows[s, pl.ds(ch, 32, stride=8), :]
    for copy in loads[3:]:
        copy.wait()

    def z1(c):
        return pltpu.make_async_remote_copy(
            mine.at[HALF * (1 - h) + c], vin.at[c, h], z1s.at[c], z1r.at[c], device_id=partner
        )

    def z1_in(c):
        return pltpu.make_async_remote_copy(
            mine.at[HALF * (1 - h) + c], vin.at[c, 1 - h], z1s.at[c], z1r.at[c], device_id=partner
        )

    def z2(c):
        return pltpu.make_async_remote_copy(
            yout.at[c, 1 - h], yrecv.at[c], z2s.at[c], z2r.at[c], device_id=partner
        )

    def member(q, side):
        x = lax.div(q, 2)
        return 4 * x + 2 * lax.rem(q, 2) + lax.rem(side + x, 2)

    def fwd(c, q):
        return pltpu.make_async_remote_copy(
            fsend.at[c, q], frecv.at[lax.div(c, 2), m], fs.at[c, q], fr.at[lax.div(c, 2), m],
            device_id={"context": 2 * member(q, lax.rem(c, 2)) + h},
        )

    def fwd_in(slot, src):
        return pltpu.make_async_remote_copy(
            fsend.at[0, 0], frecv.at[slot, src], fs.at[0, 0], fr.at[slot, src],
            device_id={"context": 2 * src + h},
        )

    def back(c, k):
        return pltpu.make_async_remote_copy(
            bsend.at[lax.div(c, 2), k], brecv.at[c, place], bs.at[lax.div(c, 2), k], br.at[c, place],
            device_id={"context": 2 * k + h},
        )

    def back_in(c, q):
        return pltpu.make_async_remote_copy(
            bsend.at[0, 0], brecv.at[c, q], bs.at[0, 0], br.at[c, q],
            device_id={"context": 2 * member(q, lax.rem(c, 2)) + h},
        )

    pl.semaphore_wait(barrier, PLANE)

    @pl.loop(0, HALF)
    def _(c):
        z1(c).start()

    @pl.loop(0, HALF)
    def _(c):
        vin[c, h] = mine[HALF * h + c]

    def forward(c):
        z1_in(c).wait_recv()
        value = jnp.concatenate(
            [jnp.concatenate([vin[c, half, s] for half in range(2)], axis=0) for s in range(3)], axis=1
        )
        part = mm(fwd1[...], tripled(value, 0))
        tr, ti = turn[0], turn[1]
        turned = []
        for s in range(3):
            re, im = part[:A, B * s : B * (s + 1)], part[A:, B * s : B * (s + 1)]
            turned.append(jnp.concatenate([re * tr - im * ti, re * ti + im * tr], axis=1))
        spec = mm(tripled(jnp.concatenate(turned, axis=0), 1), fwd2[...])
        for q in range(GROUP):
            for s in range(3):
                fsend[c, q, s] = spec[A * s + 8 * q : A * s + 8 * q + 8, :]

        @pl.loop(0, GROUP)
        def _(q):
            @pl.when(member(q, lax.rem(c, 2)) != m)
            def _():
                fwd(c, q).start()

    def middle(c):
        slot = lax.div(c, 2)
        frecv[slot, m] = fsend[c, place]

        @pl.loop(0, PLANE)
        def _(src):
            @pl.when(src != m)
            def _():
                fwd_in(slot, src).wait_recv()

        def spec(n, s):
            return frecv[slot, n, s, :, :B], frecv[slot, n, s, :, B:]

        folded = []
        for n in range(PLANE):
            re, im = spec(n, 1)
            if n + 1 < PLANE:
                next_re, next_im = spec(n + 1, 1)
                re, im = re + next_im, im - next_re
            folded.append((re, im))
        for k in range(PLANE):
            for out, s in enumerate((2, 0)):
                total_re = total_im = None
                for n in range(PLANE - k):
                    re, im = spec(n, s)
                    wr, wi = folded[n + k]
                    add_re, add_im = re * wr + im * wi, re * wi - im * wr
                    total_re = add_re if total_re is None else total_re + add_re
                    total_im = add_im if total_im is None else total_im + add_im
                bsend[slot, k, out, :, :B] = total_re
                bsend[slot, k, out, :, B:] = total_im

        @pl.loop(0, PLANE)
        def _(k):
            @pl.when(k != m)
            def _():
                back(c, k).start()

        brecv[c, place] = bsend[slot, m]

    def inverse(c):
        @pl.loop(0, GROUP)
        def _(q):
            @pl.when(member(q, lax.rem(c, 2)) != m)
            def _():
                back_in(c, q).wait_recv()

        value = jnp.concatenate([brecv[c, q, out] for out in range(2) for q in range(GROUP)], axis=0)
        part = mm(tripled(value, 1), inv1[...])
        tr, ti = turn[0], turn[1]
        turned = []
        for out in range(2):
            re, im = part[A * out : A * (out + 1), :B], part[A * out : A * (out + 1), B:]
            turned.append(jnp.concatenate([re * tr + im * ti, im * tr - re * ti], axis=0))
        y = mm(inv2[...], tripled(jnp.concatenate(turned, axis=1), 0))
        for out in range(2):
            for half in range(2):
                yout[c, half, out] = y[32 * half : 32 * (half + 1), B * out : B * (out + 1)]
        z2(c).start()

    @pl.loop(0, HALF)
    def _(c):
        forward(c)

        @pl.when(lax.rem(c, 2) == group)
        def _():
            middle(c)

        @pl.when(c > 0)
        def _():
            inverse(c - 1)

    inverse(HALF - 1)

    @pl.loop(0, HALF)
    def _(c):
        for out in range(2):
            orow[out, pl.ds(HALF * h + c, 32, stride=8), :] = yout[c, h, out]

    @pl.loop(0, HALF)
    def _(c):
        z2(c).wait_recv()
        for out in range(2):
            orow[out, pl.ds(HALF * (1 - h) + c, 32, stride=8), :] = yrecv[c, out]

    for a in range(32):
        dx_ref[:, 128 * a : 128 * a + 128] = orow[0, 8 * a : 8 * a + 8, :]
        dr_ref[:, 128 * a : 128 * a + 128] = orow[1, 8 * a : 8 * a + 8, :]

    @pl.loop(0, HALF)
    def _(c):
        z1(c).wait_send()
        z2(c).wait_send()

        @pl.loop(0, GROUP)
        def _(q):
            @pl.when(member(q, lax.rem(c, 2)) != m)
            def _():
                fwd(c, q).wait_send()

        @pl.when(lax.rem(c, 2) == group)
        def _():
            @pl.loop(0, PLANE)
            def _(k):
                @pl.when(k != m)
                def _():
                    back(c, k).wait_send()


def per_device(inputs, grads, response):
    consts = tables()
    f32, bf16 = jnp.float32, jnp.bfloat16
    vmem, dma = pltpu.VMEM, pltpu.SemaphoreType.DMA
    return pl.pallas_call(
        kernel,
        out_shape=(jax.ShapeDtypeStruct(inputs.shape, f32),) * 2,
        in_specs=[pl.BlockSpec(memory_space=pl.ANY)] * 8,
        out_specs=(pl.BlockSpec(memory_space=vmem),) * 2,
        scratch_shapes=[
            vmem((3, 8, 4096), f32),
            vmem((3, 256, 128), f32),
            vmem((8, 3, 32, 128), f32),
            vmem((HALF, 2, 3, 32, 128), f32),
            vmem((HALF, GROUP, 3, 8, 2 * B), f32),
            vmem((2, PLANE, 3, 8, 2 * B), f32),
            vmem((2, PLANE, 2, 8, 2 * B), f32),
            vmem((HALF, GROUP, 2, 8, 2 * B), f32),
            vmem((HALF, 2, 2, 32, 128), f32),
            vmem((HALF, 2, 32, 128), f32),
            vmem((2, 256, 128), f32),
            vmem((2 * A, 3 * A), bf16),
            vmem((6 * B, 2 * B), bf16),
            vmem((6 * B, 2 * B), bf16),
            vmem((A, 6 * A), bf16),
            vmem((2, A, B), f32),
            dma((8,)),
            dma((HALF,)), dma((HALF,)),
            dma((HALF, GROUP)), dma((2, PLANE)),
            dma((2, PLANE)), dma((HALF, GROUP)),
            dma((HALF,)), dma((HALF,)),
        ],
        compiler_params=pltpu.CompilerParams(collective_id=0, has_side_effects=True),
        name="hyena_backward",
    )(inputs, grads, response, *(jnp.asarray(t) for t in consts))


def solution(mesh):
    return jax.shard_map(
        per_device,
        mesh=mesh,
        in_specs=(P("tensor", "context"),) * 3,
        out_specs=(P("tensor", "context"),) * 2,
        check_vma=False,
    )
```

```python
import functools

import jax
import jax.numpy as jnp
import numpy as np
from jax import lax
from jax.experimental import pallas as pl
from jax.experimental.pallas import tpu as pltpu
from jax.sharding import PartitionSpec as P

PLANE = 16
HALF = 4
GROUP = 8
A, B = 64, 128
BLOCK = A * B
Z1_CUT = 3
Z2_CUT = 2


def split_bf16(table):
    high = table.astype(jnp.bfloat16)
    low = (table - high.astype(np.float64)).astype(jnp.bfloat16)
    return high, low


def tables():
    a, b = np.arange(A), np.arange(B)
    first = 2 * np.pi * (np.arange(A)[:, None] + 0.25) * a[None, :] / A
    last = 2 * np.pi * (np.arange(B)[:, None] * b[None, :] % B) / B
    twist = -2 * np.pi * (np.arange(A)[:, None] + 0.25) * b[None, :] / BLOCK
    fwd1 = np.concatenate([np.cos(first), -np.sin(first)], 0)
    fwd2 = np.block([[np.cos(last), -np.sin(last)], [np.sin(last), np.cos(last)]])
    inv1 = np.block([[np.cos(last), np.sin(last)], [-np.sin(last), np.cos(last)]])
    inv2 = np.concatenate([np.cos(first).T, -np.sin(first).T], 1) / BLOCK
    h, l = split_bf16(fwd1)
    fwd1 = np.concatenate([h, l, h], 1)
    h, l = split_bf16(fwd2)
    fwd2 = np.concatenate([h, l, h], 0)
    h, l = split_bf16(inv1)
    inv1 = np.concatenate([h, l, h], 0)
    h, l = split_bf16(inv2)
    inv2 = np.concatenate([h, l, h], 1)
    turn = np.stack([np.cos(twist), np.sin(twist)]).astype(np.float32)
    return fwd1, fwd2, inv1, inv2, turn


def tripled(value, axis):
    high = value.astype(jnp.bfloat16)
    low = (value - high.astype(jnp.float32)).astype(jnp.bfloat16)
    return jnp.concatenate([high, high, low], axis=axis)


def mm(left, right):
    return jnp.dot(left, right, preferred_element_type=jnp.float32)


def kernel(
    x_hbm, g_hbm, r_hbm, fwd1_hbm, fwd2_hbm, inv1_hbm, inv2_hbm, turn_hbm,
    dx_ref, dr_ref,
    raw, rows, mine, vin, fsend, frecv, bsend, brecv, yout, yrecv, orow,
    fwd1, fwd2, inv1, inv2, turn,
    in_sem, z1s, z1r, fs, fr, bs, br, z2s, z2r,
):
    ctx = lax.axis_index("context")
    h = lax.rem(ctx, 2)
    m = lax.div(ctx, 2)
    gx, gy = lax.div(m, 4), lax.rem(m, 4)
    group = lax.rem(gx + gy, 2)
    place = 2 * gx + lax.div(gy, 2)
    partner = {"context": 2 * m + 1 - h}

    barrier = pltpu.get_barrier_semaphore()
    pl.semaphore_signal(barrier, 1, device_id=partner)
    for i in range(1, PLANE):
        pl.semaphore_signal(barrier, 1, device_id={"context": 2 * lax.rem(m + i, PLANE) + h})

    loads = [
        pltpu.make_async_copy(src, dst, in_sem.at[i])
        for i, (src, dst) in enumerate(
            [(x_hbm, raw.at[0]), (g_hbm, raw.at[1]), (r_hbm, raw.at[2]),
             (fwd1_hbm, fwd1), (fwd2_hbm, fwd2), (inv1_hbm, inv1), (inv2_hbm, inv2), (turn_hbm, turn)]
        )
    ]
    for copy in loads:
        copy.start()
    for copy in loads[:3]:
        copy.wait()
    for s in range(3):
        for a in range(32):
            rows[s, 8 * a : 8 * a + 8, :] = raw[s, :, 128 * a : 128 * a + 128]
    for s in range(3):
        for ch in range(8):
            value = rows[s, pl.ds(ch, 32, stride=8), :]
            size = 96 // Z1_CUT
            for at in range(0, 32, min(32, size)):
                row = 32 * s + at
                mine[ch, row // size, row % size : row % size + min(32, size)] = value[at : at + min(32, size)]
    for copy in loads[3:]:
        copy.wait()

    def z1(c, i):
        return pltpu.make_async_remote_copy(
            mine.at[HALF * (1 - h) + c, i], vin.at[c, h, i], z1s.at[c, i], z1r.at[c, i], device_id=partner
        )

    def z1_in(c, i):
        return pltpu.make_async_remote_copy(
            mine.at[HALF * (1 - h) + c, i], vin.at[c, 1 - h, i], z1s.at[c, i], z1r.at[c, i], device_id=partner
        )

    def z2(c, i):
        return pltpu.make_async_remote_copy(
            yout.at[c, 1 - h, i], yrecv.at[c, i], z2s.at[c, i], z2r.at[c, i], device_id=partner
        )

    def member(q, side):
        x = lax.div(q, 2)
        return 4 * x + 2 * lax.rem(q, 2) + lax.rem(side + x, 2)

    def fwd(c, q):
        return pltpu.make_async_remote_copy(
            fsend.at[c, q], frecv.at[lax.div(c, 2), m], fs.at[c, q], fr.at[lax.div(c, 2), m],
            device_id={"context": 2 * member(q, lax.rem(c, 2)) + h},
        )

    def fwd_in(slot, src):
        return pltpu.make_async_remote_copy(
            fsend.at[0, 0], frecv.at[slot, src], fs.at[0, 0], fr.at[slot, src],
            device_id={"context": 2 * src + h},
        )

    def back(c, k):
        return pltpu.make_async_remote_copy(
            bsend.at[lax.div(c, 2), k], brecv.at[c, place], bs.at[lax.div(c, 2), k], br.at[c, place],
            device_id={"context": 2 * k + h},
        )

    def back_in(c, q):
        return pltpu.make_async_remote_copy(
            bsend.at[0, 0], brecv.at[c, q], bs.at[0, 0], br.at[c, q],
            device_id={"context": 2 * member(q, lax.rem(c, 2)) + h},
        )

    pl.semaphore_wait(barrier, PLANE)

    @pl.loop(0, HALF)
    def _(c):
        for i in range(Z1_CUT):
            z1(c, i).start()

    @pl.loop(0, HALF)
    def _(c):
        vin[c, h] = mine[HALF * h + c]

    def forward(c):
        for i in range(Z1_CUT):
            z1_in(c, i).wait_recv()
        value = jnp.concatenate(
            [
                jnp.concatenate([vin[c, half].reshape(96, B)[32 * s : 32 * s + 32] for half in range(2)], axis=0)
                for s in range(3)
            ],
            axis=1,
        )
        part = mm(fwd1[...], tripled(value, 0))
        tr, ti = turn[0], turn[1]
        turned = []
        for s in range(3):
            re, im = part[:A, B * s : B * (s + 1)], part[A:, B * s : B * (s + 1)]
            turned.append(jnp.concatenate([re * tr - im * ti, re * ti + im * tr], axis=1))
        spec = mm(tripled(jnp.concatenate(turned, axis=0), 1), fwd2[...])
        for q in range(GROUP):
            for s in range(3):
                fsend[c, q, s] = spec[A * s + 8 * q : A * s + 8 * q + 8, :]

        @pl.loop(0, GROUP)
        def _(q):
            @pl.when(member(q, lax.rem(c, 2)) != m)
            def _():
                fwd(c, q).start()

    def middle(c):
        slot = lax.div(c, 2)
        frecv[slot, m] = fsend[c, place]

        @pl.loop(0, PLANE)
        def _(src):
            @pl.when(src != m)
            def _():
                fwd_in(slot, src).wait_recv()

        def spec(n, s):
            return frecv[slot, n, s, :, :B], frecv[slot, n, s, :, B:]

        folded = []
        for n in range(PLANE):
            re, im = spec(n, 1)
            if n + 1 < PLANE:
                next_re, next_im = spec(n + 1, 1)
                re, im = re + next_im, im - next_re
            folded.append((re, im))
        for k in range(PLANE):
            for out, s in enumerate((2, 0)):
                total_re = total_im = None
                for n in range(PLANE - k):
                    re, im = spec(n, s)
                    wr, wi = folded[n + k]
                    add_re, add_im = re * wr + im * wi, re * wi - im * wr
                    total_re = add_re if total_re is None else total_re + add_re
                    total_im = add_im if total_im is None else total_im + add_im
                bsend[slot, k, out, :, :B] = total_re
                bsend[slot, k, out, :, B:] = total_im

        @pl.loop(0, PLANE)
        def _(k):
            @pl.when(k != m)
            def _():
                back(c, k).start()

        brecv[c, place] = bsend[slot, m]

    def inverse(c):
        @pl.loop(0, GROUP)
        def _(q):
            @pl.when(member(q, lax.rem(c, 2)) != m)
            def _():
                back_in(c, q).wait_recv()

        value = jnp.concatenate([brecv[c, q, out] for out in range(2) for q in range(GROUP)], axis=0)
        part = mm(tripled(value, 1), inv1[...])
        tr, ti = turn[0], turn[1]
        turned = []
        for out in range(2):
            re, im = part[A * out : A * (out + 1), :B], part[A * out : A * (out + 1), B:]
            turned.append(jnp.concatenate([re * tr + im * ti, im * tr - re * ti], axis=0))
        y = mm(inv2[...], tripled(jnp.concatenate(turned, axis=1), 0))
        for out in range(2):
            for half in range(2):
                size = 64 // Z2_CUT
                value = y[32 * half : 32 * (half + 1), B * out : B * (out + 1)]
                for at in range(0, 32, min(32, size)):
                    row = 32 * out + at
                    yout[c, half, row // size, row % size : row % size + min(32, size)] = value[at : at + min(32, size)]
        for i in range(Z2_CUT):
            z2(c, i).start()

    @pl.loop(0, HALF + 2)
    def _(step):
        @pl.when(step < HALF)
        def _():
            forward(step)

        @pl.when((step >= 1) & (step <= HALF) & (lax.rem(step + 1, 2) == group))
        def _():
            middle(step - 1)

        @pl.when(step >= 2)
        def _():
            inverse(step - 2)

    @pl.loop(0, HALF)
    def _(c):
        for out in range(2):
            orow[out, pl.ds(HALF * h + c, 32, stride=8), :] = yout[c, h].reshape(64, B)[32 * out : 32 * out + 32]

    @pl.loop(0, HALF)
    def _(c):
        for i in range(Z2_CUT):
            z2(c, i).wait_recv()
        for out in range(2):
            orow[out, pl.ds(HALF * (1 - h) + c, 32, stride=8), :] = yrecv[c].reshape(64, B)[32 * out : 32 * out + 32]

    for a in range(32):
        dx_ref[:, 128 * a : 128 * a + 128] = orow[0, 8 * a : 8 * a + 8, :]
        dr_ref[:, 128 * a : 128 * a + 128] = orow[1, 8 * a : 8 * a + 8, :]

    @pl.loop(0, HALF)
    def _(c):
        for i in range(Z1_CUT):
            z1(c, i).wait_send()
        for i in range(Z2_CUT):
            z2(c, i).wait_send()

        @pl.loop(0, GROUP)
        def _(q):
            @pl.when(member(q, lax.rem(c, 2)) != m)
            def _():
                fwd(c, q).wait_send()

        @pl.when(lax.rem(c, 2) == group)
        def _():
            @pl.loop(0, PLANE)
            def _(k):
                @pl.when(k != m)
                def _():
                    back(c, k).wait_send()


def per_device(inputs, grads, response):
    consts = tables()
    f32, bf16 = jnp.float32, jnp.bfloat16
    vmem, dma = pltpu.VMEM, pltpu.SemaphoreType.DMA
    return pl.pallas_call(
        kernel,
        out_shape=(jax.ShapeDtypeStruct(inputs.shape, f32),) * 2,
        in_specs=[pl.BlockSpec(memory_space=pl.ANY)] * 8,
        out_specs=(pl.BlockSpec(memory_space=vmem),) * 2,
        scratch_shapes=[
            vmem((3, 8, 4096), f32),
            vmem((3, 256, 128), f32),
            vmem((8, Z1_CUT, 96 // Z1_CUT, 128), f32),
            vmem((HALF, 2, Z1_CUT, 96 // Z1_CUT, 128), f32),
            vmem((HALF, GROUP, 3, 8, 2 * B), f32),
            vmem((2, PLANE, 3, 8, 2 * B), f32),
            vmem((2, PLANE, 2, 8, 2 * B), f32),
            vmem((HALF, GROUP, 2, 8, 2 * B), f32),
            vmem((HALF, 2, Z2_CUT, 64 // Z2_CUT, 128), f32),
            vmem((HALF, Z2_CUT, 64 // Z2_CUT, 128), f32),
            vmem((2, 256, 128), f32),
            vmem((2 * A, 3 * A), bf16),
            vmem((6 * B, 2 * B), bf16),
            vmem((6 * B, 2 * B), bf16),
            vmem((A, 6 * A), bf16),
            vmem((2, A, B), f32),
            dma((8,)),
            dma((HALF, Z1_CUT)), dma((HALF, Z1_CUT)),
            dma((HALF, GROUP)), dma((2, PLANE)),
            dma((2, PLANE)), dma((HALF, GROUP)),
            dma((HALF, Z2_CUT)), dma((HALF, Z2_CUT)),
        ],
        compiler_params=pltpu.CompilerParams(collective_id=0, has_side_effects=True),
        name="hyena_backward",
    )(inputs, grads, response, *(jnp.asarray(t) for t in consts))


def solution(mesh):
    return jax.shard_map(
        per_device,
        mesh=mesh,
        in_specs=(P("tensor", "context"),) * 3,
        out_specs=(P("tensor", "context"),) * 2,
        check_vma=False,
    )
```

```python
import functools

import jax
import jax.numpy as jnp
import numpy as np
from jax import lax
from jax.experimental import pallas as pl
from jax.experimental.pallas import tpu as pltpu
from jax.sharding import PartitionSpec as P

PLANE = 16
HALF = 4
GROUP = 8
A, B = 64, 128
BLOCK = A * B
Z1_CUT = 3
M_LAG, I_LAG = 2, 4


def split_bf16(table):
    high = table.astype(jnp.bfloat16)
    low = (table - high.astype(np.float64)).astype(jnp.bfloat16)
    return high, low


def tables():
    a, b = np.arange(A), np.arange(B)
    first = 2 * np.pi * (np.arange(A)[:, None] + 0.25) * a[None, :] / A
    last = 2 * np.pi * (np.arange(B)[:, None] * b[None, :] % B) / B
    twist = -2 * np.pi * (np.arange(A)[:, None] + 0.25) * b[None, :] / BLOCK
    fwd1 = np.concatenate([np.cos(first), -np.sin(first)], 0)
    fwd2 = np.block([[np.cos(last), -np.sin(last)], [np.sin(last), np.cos(last)]])
    inv1 = np.block([[np.cos(last), np.sin(last)], [-np.sin(last), np.cos(last)]])
    inv2 = np.concatenate([np.cos(first).T, -np.sin(first).T], 1) / BLOCK
    h, l = split_bf16(fwd1)
    fwd1 = np.concatenate([h, l, h], 1)
    h, l = split_bf16(fwd2)
    fwd2 = np.concatenate([h, l, h], 0)
    h, l = split_bf16(inv1)
    inv1 = np.concatenate([h, l, h], 0)
    h, l = split_bf16(inv2)
    inv2 = np.concatenate([h, l, h], 1)
    turn = np.stack([np.cos(twist), np.sin(twist)]).astype(np.float32)
    return fwd1, fwd2, inv1, inv2, turn


def tripled(value, axis):
    high = value.astype(jnp.bfloat16)
    low = (value - high.astype(jnp.float32)).astype(jnp.bfloat16)
    return jnp.concatenate([high, high, low], axis=axis)


def mm(left, right):
    return jnp.dot(left, right, preferred_element_type=jnp.float32)


def kernel(
    x_hbm, g_hbm, r_hbm, fwd1_hbm, fwd2_hbm, inv1_hbm, inv2_hbm, turn_hbm,
    dx_ref, dr_ref,
    raw, rows, mine, vin, fsend, frecv, bsend, brecv, yout, yrecv, orow,
    fwd1, fwd2, inv1, inv2, turn, passing,
    in_sem, z1s, z1r, ps, pr, fs, fr, bs, br, z2s, z2r,
):
    ctx = lax.axis_index("context")
    tens = lax.axis_index("tensor")
    h = ctx & 1
    m = ctx >> 1
    gx, gy = m >> 2, m & 3
    group = (gx + gy) & 1
    place = 2 * gx + (gy >> 1)
    z = 8 * h + (tens >> 1)
    partner = {"context": ctx ^ 1}

    def along_z(far):
        to = (z + far) & 15
        return {"context": 2 * m + (to >> 3), "tensor": 2 * (to & 7) + (tens & 1)}

    barrier = pltpu.get_barrier_semaphore()
    pl.semaphore_signal(barrier, 1, device_id=along_z(4))
    pl.semaphore_signal(barrier, 1, device_id=along_z(12))
    for i in range(1, PLANE):
        pl.semaphore_signal(barrier, 1, device_id={"context": 2 * ((m + i) & 15) + h})

    loads = [
        pltpu.make_async_copy(src, dst, in_sem.at[i])
        for i, (src, dst) in enumerate(
            [(x_hbm, raw.at[0]), (g_hbm, raw.at[1]), (r_hbm, raw.at[2]),
             (fwd1_hbm, fwd1), (fwd2_hbm, fwd2), (inv1_hbm, inv1), (inv2_hbm, inv2), (turn_hbm, turn)]
        )
    ]
    for copy in loads:
        copy.start()
    for copy in loads[:3]:
        copy.wait()
    for s in range(3):
        for a in range(32):
            rows[s, 8 * a : 8 * a + 8, :] = raw[s, :, 128 * a : 128 * a + 128]
    for s in range(3):
        for ch in range(8):
            mine[ch, s] = rows[s, pl.ds(ch, 32, stride=8), :]

    def way(c, i):
        return 4 + 8 * ((c + i) & 1)

    def z1(c, i):
        return pltpu.make_async_remote_copy(
            mine.at[HALF * (1 - h) + c, i], passing.at[c, i], z1s.at[c, i], pr.at[c, i], device_id=along_z(way(c, i))
        )

    def z1_on(c, i):
        side = ((z + way(c, i)) & 15) >> 3
        return pltpu.make_async_remote_copy(
            passing.at[c, i], vin.at[c, 1 - side, i], ps.at[c, i], z1r.at[c, i], device_id=along_z(way(c, i))
        )

    def z1_in(c, i):
        return pltpu.make_async_remote_copy(
            passing.at[c, i], vin.at[c, 1 - h, i], ps.at[c, i], z1r.at[c, i], device_id=along_z(way(c, i))
        )

    def z2(c, i):
        return pltpu.make_async_remote_copy(
            yout.at[c, 1 - h, i], yrecv.at[c, i], z2s.at[c, i], z2r.at[c, i], device_id=partner
        )

    def member(q, side):
        x = q >> 1
        return 4 * x + 2 * (q & 1) + ((side + x) & 1)

    def fwd(c, q):
        return pltpu.make_async_remote_copy(
            fsend.at[c, q], frecv.at[c >> 1, m], fs.at[c], fr.at[c >> 1],
            device_id={"context": 2 * member(q, c & 1) + h},
        )

    def fwd_all(c, count):
        return pltpu.make_async_remote_copy(
            fsend.at[c, pl.ds(0, count)], frecv.at[c >> 1, pl.ds(0, count)], fs.at[c], fr.at[c >> 1], device_id=partner
        )

    def fwd_in(slot):
        part = frecv.at[slot, pl.ds(0, PLANE - 1)]
        return pltpu.make_async_remote_copy(part, part, fs.at[0], fr.at[slot], device_id=partner)

    def back(c, k):
        return pltpu.make_async_remote_copy(
            bsend.at[c >> 1, k], brecv.at[c, place], bs.at[c >> 1], br.at[c], device_id={"context": 2 * k + h}
        )

    def back_in(c, count):
        part = brecv.at[c, pl.ds(0, count)]
        return pltpu.make_async_remote_copy(part, part, bs.at[0], br.at[c], device_id=partner)

    def back_out(slot):
        part = bsend.at[slot, pl.ds(0, PLANE - 1)]
        return pltpu.make_async_remote_copy(part, part, bs.at[slot], br.at[0], device_id=partner)

    pl.semaphore_wait(barrier, PLANE + 1)

    @pl.loop(0, HALF)
    def _(c):
        for i in range(Z1_CUT):
            z1(c, i).start()

    @pl.loop(0, HALF)
    def _(c):
        vin[c, h] = mine[HALF * h + c]

    for copy in loads[3:]:
        copy.wait()

    @pl.loop(0, HALF)
    def _(c):
        for i in range(Z1_CUT):
            z1(c, i).wait_recv()
            z1_on(c, i).start()

    def forward(c):
        for i in range(Z1_CUT):
            z1_in(c, i).wait_recv()
        value = jnp.concatenate(
            [jnp.concatenate([vin[c, half, s] for half in range(2)], axis=0) for s in range(3)], axis=1
        )
        part = mm(fwd1[...], tripled(value, 0))
        tr, ti = turn[0], turn[1]
        turned = []
        for s in range(3):
            re, im = part[:A, B * s : B * (s + 1)], part[A:, B * s : B * (s + 1)]
            turned.append(jnp.concatenate([re * tr - im * ti, re * ti + im * tr], axis=1))
        spec = mm(tripled(jnp.concatenate(turned, axis=0), 1), fwd2[...])
        for q in range(GROUP):
            for s in range(3):
                fsend[c, q, s] = spec[A * s + 8 * q : A * s + 8 * q + 8, :]

        for i in range(1, GROUP):
            fwd(c, (place + i) & 7).start()

        @pl.when((c & 1) != group)
        def _():
            fwd(c, place).start()

    def middle(c):
        slot = c >> 1
        frecv[slot, m] = fsend[c, place]
        fwd_in(slot).wait_recv()

        def spec(n, s):
            return frecv[slot, n, s, :, :B], frecv[slot, n, s, :, B:]

        folded = []
        for n in range(PLANE):
            re, im = spec(n, 1)
            if n + 1 < PLANE:
                next_re, next_im = spec(n + 1, 1)
                re, im = re + next_im, im - next_re
            folded.append((re, im))
        for k in range(PLANE):
            for out, s in enumerate((2, 0)):
                total_re = total_im = None
                for n in range(PLANE - k):
                    re, im = spec(n, s)
                    wr, wi = folded[n + k]
                    add_re, add_im = re * wr + im * wi, re * wi - im * wr
                    total_re = add_re if total_re is None else total_re + add_re
                    total_im = add_im if total_im is None else total_im + add_im
                bsend[slot, k, out, :, :B] = total_re
                bsend[slot, k, out, :, B:] = total_im
        for i in range(1, PLANE):
            back(c, (m + i) & 15).start()
        brecv[c, place] = bsend[slot, m]

    def inverse(c):
        @pl.when((c & 1) == group)
        def _():
            back_in(c, GROUP - 1).wait_recv()

        @pl.when((c & 1) != group)
        def _():
            back_in(c, GROUP).wait_recv()

        value = jnp.concatenate([brecv[c, q, out] for out in range(2) for q in range(GROUP)], axis=0)
        part = mm(tripled(value, 1), inv1[...])
        tr, ti = turn[0], turn[1]
        turned = []
        for out in range(2):
            re, im = part[A * out : A * (out + 1), :B], part[A * out : A * (out + 1), B:]
            turned.append(jnp.concatenate([re * tr + im * ti, im * tr - re * ti], axis=0))
        y = mm(inv2[...], tripled(jnp.concatenate(turned, axis=1), 0))
        for out in range(2):
            for half in range(2):
                yout[c, half, out] = y[32 * half : 32 * (half + 1), B * out : B * (out + 1)]
        for i in range(2):
            z2(c, i).start()

    @pl.loop(0, HALF + I_LAG)
    def _(step):
        @pl.when(step < HALF)
        def _():
            forward(step)

        @pl.when((step >= M_LAG) & (step < HALF + M_LAG) & (((step + M_LAG) & 1) == group))
        def _():
            middle(step - M_LAG)

        @pl.when(step >= I_LAG)
        def _():
            inverse(step - I_LAG)

    @pl.loop(0, HALF)
    def _(c):
        for i in range(Z1_CUT):
            z1(c, i).wait_send()
            z1_on(c, i).wait_send()

        @pl.when((c & 1) == group)
        def _():
            fwd_all(c, GROUP - 1).wait_send()
            back_out(c >> 1).wait_send()

        @pl.when((c & 1) != group)
        def _():
            fwd_all(c, GROUP).wait_send()

        for out in range(2):
            orow[out, pl.ds(HALF * h + c, 32, stride=8), :] = yout[c, h, out]

    @pl.loop(0, HALF)
    def _(c):
        for i in range(2):
            z2(c, i).wait_recv()
            orow[i, pl.ds(HALF * (1 - h) + c, 32, stride=8), :] = yrecv[c, i]

    for a in range(32):
        dx_ref[:, 128 * a : 128 * a + 128] = orow[0, 8 * a : 8 * a + 8, :]
        dr_ref[:, 128 * a : 128 * a + 128] = orow[1, 8 * a : 8 * a + 8, :]

    @pl.loop(0, HALF)
    def _(c):
        for i in range(2):
            z2(c, i).wait_send()


def per_device(inputs, grads, response):
    consts = tables()
    f32, bf16 = jnp.float32, jnp.bfloat16
    vmem, dma = pltpu.VMEM, pltpu.SemaphoreType.DMA
    return pl.pallas_call(
        kernel,
        out_shape=(jax.ShapeDtypeStruct(inputs.shape, f32),) * 2,
        in_specs=[pl.BlockSpec(memory_space=pl.ANY)] * 8,
        out_specs=(pl.BlockSpec(memory_space=vmem),) * 2,
        scratch_shapes=[
            vmem((3, 8, 4096), f32),
            vmem((3, 256, 128), f32),
            vmem((8, Z1_CUT, 32, 128), f32),
            vmem((HALF, 2, Z1_CUT, 32, 128), f32),
            vmem((HALF, GROUP, 3, 8, 2 * B), f32),
            vmem((2, PLANE, 3, 8, 2 * B), f32),
            vmem((2, PLANE, 2, 8, 2 * B), f32),
            vmem((HALF, GROUP, 2, 8, 2 * B), f32),
            vmem((HALF, 2, 2, 32, 128), f32),
            vmem((HALF, 2, 32, 128), f32),
            vmem((2, 256, 128), f32),
            vmem((2 * A, 3 * A), bf16),
            vmem((6 * B, 2 * B), bf16),
            vmem((6 * B, 2 * B), bf16),
            vmem((A, 6 * A), bf16),
            vmem((2, A, B), f32),
            vmem((HALF, Z1_CUT, 32, B), f32),
            dma((8,)),
            dma((HALF, Z1_CUT)), dma((HALF, Z1_CUT)),
            dma((HALF, Z1_CUT)), dma((HALF, Z1_CUT)),
            dma((HALF,)), dma((2,)),
            dma((2,)), dma((HALF,)),
            dma((HALF, 2)), dma((HALF, 2)),
        ],
        compiler_params=pltpu.CompilerParams(collective_id=0, has_side_effects=True),
        name="hyena_backward",
    )(inputs, grads, response, *(jnp.asarray(t) for t in consts))


def solution(mesh):
    return jax.shard_map(
        per_device,
        mesh=mesh,
        in_specs=(P("tensor", "context"),) * 3,
        out_specs=(P("tensor", "context"),) * 2,
        check_vma=False,
    )
```

```python
import functools

import jax
import jax.numpy as jnp
import numpy as np
from jax import lax
from jax.experimental import pallas as pl
from jax.experimental.pallas import tpu as pltpu
from jax.sharding import PartitionSpec as P

PLANE = 16
HALF = 4
GROUP = 8
A, B = 64, 128
BLOCK = A * B
Z1_CUT = 3
I_LAG = 2


def split_bf16(table):
    high = table.astype(jnp.bfloat16)
    low = (table - high.astype(np.float64)).astype(jnp.bfloat16)
    return high, low


def tables():
    a, b = np.arange(A), np.arange(B)
    first = 2 * np.pi * (np.arange(A)[:, None] + 0.25) * a[None, :] / A
    last = 2 * np.pi * (np.arange(B)[:, None] * b[None, :] % B) / B
    twist = -2 * np.pi * (np.arange(A)[:, None] + 0.25) * b[None, :] / BLOCK
    fwd1 = np.concatenate([np.cos(first), -np.sin(first)], 0)
    fwd2 = np.block([[np.cos(last), -np.sin(last)], [np.sin(last), np.cos(last)]])
    inv1 = np.block([[np.cos(last), np.sin(last)], [-np.sin(last), np.cos(last)]])
    inv2 = np.concatenate([np.cos(first).T, -np.sin(first).T], 1) / BLOCK
    h, l = split_bf16(fwd1)
    fwd1 = np.concatenate([h, l, h], 1)
    h, l = split_bf16(fwd2)
    fwd2 = np.concatenate([h, l, h], 0)
    h, l = split_bf16(inv1)
    inv1 = np.concatenate([h, l, h], 0)
    h, l = split_bf16(inv2)
    inv2 = np.concatenate([h, l, h], 1)
    turn = np.stack([np.cos(twist), np.sin(twist)]).astype(np.float32)
    return fwd1, fwd2, inv1, inv2, turn


def tripled(value, axis):
    high = value.astype(jnp.bfloat16)
    low = (value - high.astype(jnp.float32)).astype(jnp.bfloat16)
    return jnp.concatenate([high, high, low], axis=axis)


def mm(left, right):
    return jnp.dot(left, right, preferred_element_type=jnp.float32)


def kernel(
    x_hbm, g_hbm, r_hbm, fwd1_hbm, fwd2_hbm, inv1_hbm, inv2_hbm, turn_hbm,
    yout, yrecv,
    raw, rows, mine, vin, fsend, frecv, bsend, brecv, ybuf,
    fwd1, fwd2, inv1, inv2, turn, passing,
    in_sem, z1s, z1r, ps, pr, fs, fr, bs, br, z2s, z2r, ready,
):
    ctx = lax.axis_index("context")
    tens = lax.axis_index("tensor")
    h = ctx & 1
    m = ctx >> 1
    gx, gy = m >> 2, m & 3
    group = (gx + gy) & 1
    place = 2 * gx + (gy >> 1)
    z = 8 * h + (tens >> 1)
    partner = {"context": ctx ^ 1}

    def row_peer(i):
        return {"context": 2 * ((m & 12) + ((m + i) & 3)) + h}

    def along_z(far):
        to = (z + far) & 15
        return {"context": 2 * m + (to >> 3), "tensor": 2 * (to & 7) + (tens & 1)}

    loads = [
        pltpu.make_async_copy(src, dst, in_sem.at[i])
        for i, (src, dst) in enumerate(
            [(x_hbm, raw.at[0]), (g_hbm, raw.at[1]), (r_hbm, raw.at[2]),
             (fwd1_hbm, fwd1), (fwd2_hbm, fwd2), (inv1_hbm, inv1), (inv2_hbm, inv2), (turn_hbm, turn)]
        )
    ]
    for copy in loads[:3]:
        copy.start()
    barrier = pltpu.get_barrier_semaphore()
    pl.semaphore_signal(barrier, 1, device_id=along_z(4))
    pl.semaphore_signal(barrier, 1, device_id=along_z(12))
    for i in range(1, 4):
        pl.semaphore_signal(barrier, 1, device_id={"context": 2 * ((m + 4 * i) & 15) + h})
        pl.semaphore_signal(barrier, 1, device_id=row_peer(i))
    for s in range(3):
        loads[s].wait()
        for a in range(32):
            rows[s, 8 * a : 8 * a + 8, :] = raw[s, :, 128 * a : 128 * a + 128]
        for c in range(HALF):
            mine[c, s] = rows[s, pl.ds(HALF * (1 - h) + c, 32, stride=8), :]

    def way(c, i):
        return 4 + 8 * ((c + i) & 1)

    def z1(c, i):
        return pltpu.make_async_remote_copy(
            mine.at[c, i], passing.at[c, i], z1s.at[c, i], pr.at[c, i], device_id=along_z(way(c, i))
        )

    def z1_on(c, i):
        side = ((z + way(c, i)) & 15) >> 3
        return pltpu.make_async_remote_copy(
            passing.at[c, i], vin.at[c, 1 - side, i], ps.at[c, i], z1r.at[c, i], device_id=along_z(way(c, i))
        )

    def z1_in(c, i):
        return pltpu.make_async_remote_copy(
            passing.at[c, i], vin.at[c, 1 - h, i], ps.at[c, i], z1r.at[c, i], device_id=along_z(way(c, i))
        )

    def z2(c, i):
        return pltpu.make_async_remote_copy(
            ybuf.at[c, 1 - h, i], yrecv.at[c, i], z2s.at[c, i], z2r.at[c, i], device_id=partner
        )

    def member(q, side):
        x = q >> 1
        return 4 * x + 2 * (q & 1) + ((side + x) & 1)

    def fwd(c, q):
        return pltpu.make_async_remote_copy(
            fsend.at[c, q], frecv.at[c >> 1, m], fs.at[c], fr.at[c >> 1],
            device_id={"context": 2 * member(q, c & 1) + h},
        )

    def fwd_all(c, count):
        return pltpu.make_async_remote_copy(
            fsend.at[c, pl.ds(0, count)], frecv.at[c >> 1, pl.ds(0, count)], fs.at[c], fr.at[c >> 1], device_id=partner
        )

    def fwd_in(slot):
        part = frecv.at[slot, pl.ds(0, PLANE - 1)]
        return pltpu.make_async_remote_copy(part, part, fs.at[0], fr.at[slot], device_id=partner)

    def back(c, k):
        return pltpu.make_async_remote_copy(
            bsend.at[c >> 1, k], brecv.at[c, place], bs.at[c >> 1], br.at[c], device_id={"context": 2 * k + h}
        )

    def back_in(c, count):
        part = brecv.at[c, pl.ds(0, count)]
        return pltpu.make_async_remote_copy(part, part, bs.at[0], br.at[c], device_id=partner)

    def back_out(slot):
        part = bsend.at[slot, pl.ds(0, PLANE - 1)]
        return pltpu.make_async_remote_copy(part, part, bs.at[slot], br.at[0], device_id=partner)

    pl.semaphore_wait(barrier, 8)

    @pl.loop(0, HALF)
    def _(c):
        for i in range(Z1_CUT):
            z1(c, i).start()

    for i in range(1, 4):
        pl.semaphore_signal(ready, 1, device_id=row_peer(i))
    for copy in loads[3:]:
        copy.start()
    for s in range(3):
        for c in range(HALF):
            vin[c, h, s] = rows[s, pl.ds(HALF * h + c, 32, stride=8), :]
    for copy in loads[3:]:
        copy.wait()

    @pl.loop(0, HALF)
    def _(c):
        for i in range(Z1_CUT):
            z1(c, i).wait_recv()
            z1_on(c, i).start()

    pl.semaphore_wait(ready, 3)

    def forward(c):
        for i in range(Z1_CUT):
            z1_in(c, i).wait_recv()
        value = jnp.concatenate(
            [jnp.concatenate([vin[c, half, s] for half in range(2)], axis=0) for s in range(3)], axis=1
        )
        part = mm(fwd1[...], tripled(value, 0))
        tr, ti = turn[0], turn[1]
        turned = []
        for s in range(3):
            re, im = part[:A, B * s : B * (s + 1)], part[A:, B * s : B * (s + 1)]
            turned.append(jnp.concatenate([re * tr - im * ti, re * ti + im * tr], axis=1))
        spec = mm(tripled(jnp.concatenate(turned, axis=0), 1), fwd2[...])
        for q in range(GROUP):
            for s in range(3):
                fsend[c, q, s] = spec[A * s + 8 * q : A * s + 8 * q + 8, :]

        for i in range(1, GROUP):
            fwd(c, (place + i) & 7).start()

        @pl.when((c & 1) != group)
        def _():
            fwd(c, place).start()

    def middle(c):
        slot = c >> 1
        frecv[slot, m] = fsend[c, place]
        fwd_in(slot).wait_recv()

        def spec(n, s):
            return frecv[slot, n, s, :, :B], frecv[slot, n, s, :, B:]

        folded = []
        for n in range(PLANE):
            re, im = spec(n, 1)
            if n + 1 < PLANE:
                next_re, next_im = spec(n + 1, 1)
                re, im = re + next_im, im - next_re
            folded.append((re, im))
        for k in range(PLANE):
            for out, s in enumerate((2, 0)):
                total_re = total_im = None
                for n in range(PLANE - k):
                    re, im = spec(n, s)
                    wr, wi = folded[n + k]
                    add_re, add_im = re * wr + im * wi, re * wi - im * wr
                    total_re = add_re if total_re is None else total_re + add_re
                    total_im = add_im if total_im is None else total_im + add_im
                bsend[slot, k, out, :, :B] = total_re
                bsend[slot, k, out, :, B:] = total_im
        for i in range(1, PLANE):
            back(c, (m + i) & 15).start()
        brecv[c, place] = bsend[slot, m]

    def inverse(c):
        @pl.when((c & 1) == group)
        def _():
            back_in(c, GROUP - 1).wait_recv()

        @pl.when((c & 1) != group)
        def _():
            back_in(c, GROUP).wait_recv()

        value = jnp.concatenate([brecv[c, q, out] for out in range(2) for q in range(GROUP)], axis=0)
        part = mm(tripled(value, 1), inv1[...])
        tr, ti = turn[0], turn[1]
        turned = []
        for out in range(2):
            re, im = part[A * out : A * (out + 1), :B], part[A * out : A * (out + 1), B:]
            turned.append(jnp.concatenate([re * tr + im * ti, im * tr - re * ti], axis=0))
        y = mm(inv2[...], tripled(jnp.concatenate(turned, axis=1), 0))
        for out in range(2):
            for half in range(2):
                ybuf[c, half, out] = y[32 * half : 32 * (half + 1), B * out : B * (out + 1)]
        for i in range(2):
            z2(c, i).start()

    @pl.loop(0, HALF)
    def _(c):
        forward(c)

    @pl.loop(0, HALF + I_LAG)
    def _(step):
        @pl.when((step < HALF) & ((step & 1) == group))
        def _():
            middle(step)

        @pl.when(step >= I_LAG)
        def _():
            inverse(step - I_LAG)

    @pl.loop(0, HALF)
    def _(c):
        for i in range(Z1_CUT):
            z1(c, i).wait_send()
            z1_on(c, i).wait_send()

        @pl.when((c & 1) == group)
        def _():
            fwd_all(c, GROUP - 1).wait_send()
            back_out(c >> 1).wait_send()

        @pl.when((c & 1) != group)
        def _():
            fwd_all(c, GROUP).wait_send()

    own = [pltpu.make_async_copy(ybuf.at[c, h], yout.at[c], in_sem.at[c]) for c in range(HALF)]
    for copy in own:
        copy.start()
    for copy in own:
        copy.wait()

    @pl.loop(0, HALF)
    def _(c):
        for i in range(2):
            z2(c, i).wait()


def arrange(own_hbm, other_hbm, dx_ref, dr_ref, own, other, sem):
    h = lax.axis_index("context") & 1
    copies = [pltpu.make_async_copy(own_hbm, own, sem.at[0]), pltpu.make_async_copy(other_hbm, other, sem.at[1])]
    for copy in copies:
        copy.start()
    for copy in copies:
        copy.wait()
    for out, ref in enumerate((dx_ref, dr_ref)):
        low = [jnp.where(h == 0, own[c, out], other[c, out]) for c in range(HALF)]
        high = [jnp.where(h == 0, other[c, out], own[c, out]) for c in range(HALF)]
        turned = jnp.stack(low + high, axis=1)
        for a in range(32):
            ref[:, 128 * a : 128 * a + 128] = turned[a]


def per_device(inputs, grads, response):
    consts = tables()
    f32, bf16 = jnp.float32, jnp.bfloat16
    vmem, dma = pltpu.VMEM, pltpu.SemaphoreType.DMA
    own, other = pl.pallas_call(
        kernel,
        out_shape=(jax.ShapeDtypeStruct((HALF, 2, 32, B), f32),) * 2,
        in_specs=[pl.BlockSpec(memory_space=pl.ANY)] * 8,
        out_specs=(pl.BlockSpec(memory_space=pl.ANY),) * 2,
        scratch_shapes=[
            vmem((3, 8, 4096), f32),
            vmem((3, 256, 128), f32),
            vmem((HALF, Z1_CUT, 32, 128), f32),
            vmem((HALF, 2, Z1_CUT, 32, 128), f32),
            vmem((HALF, GROUP, 3, 8, 2 * B), f32),
            vmem((2, PLANE, 3, 8, 2 * B), f32),
            vmem((2, PLANE, 2, 8, 2 * B), f32),
            vmem((HALF, GROUP, 2, 8, 2 * B), f32),
            vmem((HALF, 2, 2, 32, 128), f32),
            vmem((2 * A, 3 * A), bf16),
            vmem((6 * B, 2 * B), bf16),
            vmem((6 * B, 2 * B), bf16),
            vmem((A, 6 * A), bf16),
            vmem((2, A, B), f32),
            vmem((HALF, Z1_CUT, 32, B), f32),
            dma((8,)),
            dma((HALF, Z1_CUT)), dma((HALF, Z1_CUT)),
            dma((HALF, Z1_CUT)), dma((HALF, Z1_CUT)),
            dma((HALF,)), dma((2,)),
            dma((2,)), dma((HALF,)),
            dma((HALF, 2)), dma((HALF, 2)),
            pltpu.SemaphoreType.REGULAR,
        ],
        compiler_params=pltpu.CompilerParams(collective_id=0, has_side_effects=True),
        name="hyena_backward",
    )(inputs, grads, response, *(jnp.asarray(t) for t in consts))
    return pl.pallas_call(
        arrange,
        out_shape=(jax.ShapeDtypeStruct(inputs.shape, f32),) * 2,
        in_specs=[pl.BlockSpec(memory_space=pl.ANY)] * 2,
        out_specs=(pl.BlockSpec(memory_space=vmem),) * 2,
        scratch_shapes=[vmem((HALF, 2, 32, B), f32), vmem((HALF, 2, 32, B), f32), dma((2,))],
        name="arrange",
    )(own, other)


def solution(mesh):
    return jax.shard_map(
        per_device,
        mesh=mesh,
        in_specs=(P("tensor", "context"),) * 3,
        out_specs=(P("tensor", "context"),) * 2,
        check_vma=False,
    )
```

```python
import functools

import jax
import jax.numpy as jnp
import numpy as np
from jax import lax
from jax.experimental import pallas as pl
from jax.experimental.pallas import tpu as pltpu
from jax.sharding import PartitionSpec as P

PLANE = 16
HALF = 4
GROUP = 8
A, B = 64, 128
BLOCK = A * B
Z1_CUT = 3
I_LAG = 3


def split_bf16(table):
    high = table.astype(jnp.bfloat16)
    low = (table - high.astype(np.float64)).astype(jnp.bfloat16)
    return high, low


def tables():
    a, b = np.arange(A), np.arange(B)
    first = 2 * np.pi * (np.arange(A)[:, None] + 0.25) * a[None, :] / A
    last = 2 * np.pi * (np.arange(B)[:, None] * b[None, :] % B) / B
    twist = -2 * np.pi * (np.arange(A)[:, None] + 0.25) * b[None, :] / BLOCK
    fwd1 = np.concatenate([np.cos(first), -np.sin(first)], 0)
    fwd2 = np.block([[np.cos(last), -np.sin(last)], [np.sin(last), np.cos(last)]])
    inv1 = np.block([[np.cos(last), np.sin(last)], [-np.sin(last), np.cos(last)]])
    inv2 = np.concatenate([np.cos(first).T, -np.sin(first).T], 1) / BLOCK
    h, l = split_bf16(fwd1)
    fwd1 = np.concatenate([h, l, h], 1)
    h, l = split_bf16(fwd2)
    fwd2 = np.concatenate([h, l, h], 0)
    h, l = split_bf16(inv1)
    inv1 = np.concatenate([h, l, h], 0)
    h, l = split_bf16(inv2)
    inv2 = np.concatenate([h, l, h], 1)
    turn = np.stack([np.cos(twist), np.sin(twist)]).astype(np.float32)
    return fwd1, fwd2, inv1, inv2, turn


def tripled(value, axis):
    high = value.astype(jnp.bfloat16)
    low = (value - high.astype(jnp.float32)).astype(jnp.bfloat16)
    return jnp.concatenate([high, high, low], axis=axis)


def mm(left, right):
    return jnp.dot(left, right, preferred_element_type=jnp.float32)


def kernel(
    x_hbm, g_hbm, r_hbm, fwd1_hbm, fwd2_hbm, inv1_hbm, inv2_hbm, turn_hbm,
    yout, yrecv,
    raw, rows, mine, vin, fsend, frecv, bsend, brecv, ybuf,
    fwd1, fwd2, inv1, inv2, turn, passing,
    in_sem, z1s, z1r, ps, pr, fs, fr, bs, br, z2s, z2r, ready,
):
    ctx = lax.axis_index("context")
    tens = lax.axis_index("tensor")
    h = ctx & 1
    m = ctx >> 1
    gx, gy = m >> 2, m & 3
    group = (gx + gy) & 1
    place = 2 * gx + (gy >> 1)
    z = 8 * h + (tens >> 1)
    partner = {"context": ctx ^ 1}

    def row_peer(i):
        return {"context": 2 * ((m & 12) + ((m + i) & 3)) + h}

    def along_z(far):
        to = (z + far) & 15
        return {"context": 2 * m + (to >> 3), "tensor": 2 * (to & 7) + (tens & 1)}

    loads = [
        pltpu.make_async_copy(src, dst, in_sem.at[i])
        for i, (src, dst) in enumerate(
            [(x_hbm, raw.at[0]), (g_hbm, raw.at[1]), (r_hbm, raw.at[2]),
             (fwd1_hbm, fwd1), (fwd2_hbm, fwd2), (inv1_hbm, inv1), (inv2_hbm, inv2), (turn_hbm, turn)]
        )
    ]
    for copy in loads[:3]:
        copy.start()
    barrier = pltpu.get_barrier_semaphore()
    pl.semaphore_signal(barrier, 1, device_id=along_z(4))
    pl.semaphore_signal(barrier, 1, device_id=along_z(12))
    for i in range(1, 4):
        pl.semaphore_signal(barrier, 1, device_id={"context": 2 * ((m + 4 * i) & 15) + h})
        pl.semaphore_signal(barrier, 1, device_id=row_peer(i))
    for s in range(3):
        loads[s].wait()
        for a in range(32):
            rows[s, 8 * a : 8 * a + 8, :] = raw[s, :, 128 * a : 128 * a + 128]
        for c in range(HALF):
            mine[c, s] = rows[s, pl.ds(HALF * (1 - h) + c, 32, stride=8), :]

    def way(c, i):
        return 4 + 8 * ((c + i) & 1)

    def z1(c, i):
        return pltpu.make_async_remote_copy(
            mine.at[c, i], passing.at[c, i], z1s.at[c, i], pr.at[c, i], device_id=along_z(way(c, i))
        )

    def z1_on(c, i):
        side = ((z + way(c, i)) & 15) >> 3
        return pltpu.make_async_remote_copy(
            passing.at[c, i], vin.at[c, 1 - side, i], ps.at[c, i], z1r.at[c, i], device_id=along_z(way(c, i))
        )

    def z1_in(c, i):
        return pltpu.make_async_remote_copy(
            passing.at[c, i], vin.at[c, 1 - h, i], ps.at[c, i], z1r.at[c, i], device_id=along_z(way(c, i))
        )

    def z2(c, i):
        return pltpu.make_async_remote_copy(
            ybuf.at[c, 1 - h, i], yrecv.at[c, i], z2s.at[c, i], z2r.at[c, i], device_id=partner
        )

    def member(q, side):
        x = q >> 1
        return 4 * x + 2 * (q & 1) + ((side + x) & 1)

    def fwd(c, q):
        return pltpu.make_async_remote_copy(
            fsend.at[c, q], frecv.at[c >> 1, m], fs.at[c], fr.at[c >> 1],
            device_id={"context": 2 * member(q, c & 1) + h},
        )

    def fwd_all(c, count):
        return pltpu.make_async_remote_copy(
            fsend.at[c, pl.ds(0, count)], frecv.at[c >> 1, pl.ds(0, count)], fs.at[c], fr.at[c >> 1], device_id=partner
        )

    def fwd_in(slot):
        part = frecv.at[slot, pl.ds(0, PLANE - 1)]
        return pltpu.make_async_remote_copy(part, part, fs.at[0], fr.at[slot], device_id=partner)

    def back(c, k):
        return pltpu.make_async_remote_copy(
            bsend.at[c >> 1, k], brecv.at[c, place], bs.at[c >> 1], br.at[c], device_id={"context": 2 * k + h}
        )

    def back_in(c, count):
        part = brecv.at[c, pl.ds(0, count)]
        return pltpu.make_async_remote_copy(part, part, bs.at[0], br.at[c], device_id=partner)

    def back_out(slot):
        part = bsend.at[slot, pl.ds(0, PLANE - 1)]
        return pltpu.make_async_remote_copy(part, part, bs.at[slot], br.at[0], device_id=partner)

    pl.semaphore_wait(barrier, 8)

    @pl.loop(0, HALF)
    def _(c):
        for i in range(Z1_CUT):
            z1(c, i).start()

    for i in range(1, 4):
        pl.semaphore_signal(ready, 1, device_id=row_peer(i))
    for copy in loads[3:]:
        copy.start()
    for s in range(3):
        for c in range(HALF):
            vin[c, h, s] = rows[s, pl.ds(HALF * h + c, 32, stride=8), :]
    for copy in loads[3:]:
        copy.wait()

    @pl.loop(0, HALF)
    def _(c):
        for i in range(Z1_CUT):
            z1(c, i).wait_recv()
            z1_on(c, i).start()

    pl.semaphore_wait(ready, 3)

    def forward(c):
        for i in range(Z1_CUT):
            z1_in(c, i).wait_recv()
        value = jnp.concatenate(
            [jnp.concatenate([vin[c, half, s] for half in range(2)], axis=0) for s in range(3)], axis=1
        )
        part = mm(fwd1[...], tripled(value, 0))
        tr, ti = turn[0], turn[1]
        turned = []
        for s in range(3):
            re, im = part[:A, B * s : B * (s + 1)], part[A:, B * s : B * (s + 1)]
            turned.append(jnp.concatenate([re * tr - im * ti, re * ti + im * tr], axis=1))
        spec = mm(tripled(jnp.concatenate(turned, axis=0), 1), fwd2[...])
        for q in range(GROUP):
            for s in range(3):
                fsend[c, q, s] = spec[A * s + 8 * q : A * s + 8 * q + 8, :]

        for i in range(1, GROUP):
            fwd(c, (place + i) & 7).start()

        @pl.when((c & 1) != group)
        def _():
            fwd(c, place).start()

    def middle(c):
        slot = c >> 1
        frecv[slot, m] = fsend[c, place]
        fwd_in(slot).wait_recv()

        def spec(n, s):
            return frecv[slot, n, s, :, :B], frecv[slot, n, s, :, B:]

        folded = []
        for n in range(PLANE):
            re, im = spec(n, 1)
            if n + 1 < PLANE:
                next_re, next_im = spec(n + 1, 1)
                re, im = re + next_im, im - next_re
            folded.append((re, im))
        for k in range(PLANE):
            for out, s in enumerate((2, 0)):
                total_re = total_im = None
                for n in range(PLANE - k):
                    re, im = spec(n, s)
                    wr, wi = folded[n + k]
                    add_re, add_im = re * wr + im * wi, re * wi - im * wr
                    total_re = add_re if total_re is None else total_re + add_re
                    total_im = add_im if total_im is None else total_im + add_im
                bsend[slot, k, out, :, :B] = total_re
                bsend[slot, k, out, :, B:] = total_im

            @pl.when(m != k)
            def _(k=k):
                back(c, k).start()

        brecv[c, place] = bsend[slot, m]

    def inverse(c):
        @pl.when((c & 1) == group)
        def _():
            back_in(c, GROUP - 1).wait_recv()

        @pl.when((c & 1) != group)
        def _():
            back_in(c, GROUP).wait_recv()

        value = jnp.concatenate([brecv[c, q, out] for out in range(2) for q in range(GROUP)], axis=0)
        part = mm(tripled(value, 1), inv1[...])
        tr, ti = turn[0], turn[1]
        turned = []
        for out in range(2):
            re, im = part[A * out : A * (out + 1), :B], part[A * out : A * (out + 1), B:]
            turned.append(jnp.concatenate([re * tr + im * ti, im * tr - re * ti], axis=0))
        y = mm(inv2[...], tripled(jnp.concatenate(turned, axis=1), 0))
        for out in range(2):
            for half in range(2):
                ybuf[c, half, out] = y[32 * half : 32 * (half + 1), B * out : B * (out + 1)]
        for i in range(2):
            z2(c, i).start()

    @pl.loop(0, HALF)
    def _(c):
        forward(c)

    @pl.loop(0, HALF + I_LAG)
    def _(step):
        @pl.when((step < HALF) & ((step & 1) == group))
        def _():
            middle(step)

        @pl.when(step >= I_LAG)
        def _():
            inverse(step - I_LAG)

    @pl.loop(0, HALF)
    def _(c):
        for i in range(Z1_CUT):
            z1(c, i).wait_send()
            z1_on(c, i).wait_send()

        @pl.when((c & 1) == group)
        def _():
            fwd_all(c, GROUP - 1).wait_send()
            back_out(c >> 1).wait_send()

        @pl.when((c & 1) != group)
        def _():
            fwd_all(c, GROUP).wait_send()

    own = [pltpu.make_async_copy(ybuf.at[c, h], yout.at[c], in_sem.at[c]) for c in range(HALF)]
    for copy in own:
        copy.start()
    for copy in own:
        copy.wait()

    @pl.loop(0, HALF)
    def _(c):
        for i in range(2):
            z2(c, i).wait()


def arrange(own_hbm, other_hbm, dx_ref, dr_ref, own, other, sem):
    h = lax.axis_index("context") & 1
    copies = [pltpu.make_async_copy(own_hbm, own, sem.at[0]), pltpu.make_async_copy(other_hbm, other, sem.at[1])]
    for copy in copies:
        copy.start()
    for copy in copies:
        copy.wait()
    for out, ref in enumerate((dx_ref, dr_ref)):
        low = [jnp.where(h == 0, own[c, out], other[c, out]) for c in range(HALF)]
        high = [jnp.where(h == 0, other[c, out], own[c, out]) for c in range(HALF)]
        turned = jnp.stack(low + high, axis=1)
        for a in range(32):
            ref[:, 128 * a : 128 * a + 128] = turned[a]


def per_device(inputs, grads, response):
    consts = tables()
    f32, bf16 = jnp.float32, jnp.bfloat16
    vmem, dma = pltpu.VMEM, pltpu.SemaphoreType.DMA
    own, other = pl.pallas_call(
        kernel,
        out_shape=(jax.ShapeDtypeStruct((HALF, 2, 32, B), f32),) * 2,
        in_specs=[pl.BlockSpec(memory_space=pl.ANY)] * 8,
        out_specs=(pl.BlockSpec(memory_space=pl.ANY),) * 2,
        scratch_shapes=[
            vmem((3, 8, 4096), f32),
            vmem((3, 256, 128), f32),
            vmem((HALF, Z1_CUT, 32, 128), f32),
            vmem((HALF, 2, Z1_CUT, 32, 128), f32),
            vmem((HALF, GROUP, 3, 8, 2 * B), f32),
            vmem((2, PLANE, 3, 8, 2 * B), f32),
            vmem((2, PLANE, 2, 8, 2 * B), f32),
            vmem((HALF, GROUP, 2, 8, 2 * B), f32),
            vmem((HALF, 2, 2, 32, 128), f32),
            vmem((2 * A, 3 * A), bf16),
            vmem((6 * B, 2 * B), bf16),
            vmem((6 * B, 2 * B), bf16),
            vmem((A, 6 * A), bf16),
            vmem((2, A, B), f32),
            vmem((HALF, Z1_CUT, 32, B), f32),
            dma((8,)),
            dma((HALF, Z1_CUT)), dma((HALF, Z1_CUT)),
            dma((HALF, Z1_CUT)), dma((HALF, Z1_CUT)),
            dma((HALF,)), dma((2,)),
            dma((2,)), dma((HALF,)),
            dma((HALF, 2)), dma((HALF, 2)),
            pltpu.SemaphoreType.REGULAR,
        ],
        compiler_params=pltpu.CompilerParams(collective_id=0, has_side_effects=True),
        name="hyena_backward",
    )(inputs, grads, response, *(jnp.asarray(t) for t in consts))
    return pl.pallas_call(
        arrange,
        out_shape=(jax.ShapeDtypeStruct(inputs.shape, f32),) * 2,
        in_specs=[pl.BlockSpec(memory_space=pl.ANY)] * 2,
        out_specs=(pl.BlockSpec(memory_space=vmem),) * 2,
        scratch_shapes=[vmem((HALF, 2, 32, B), f32), vmem((HALF, 2, 32, B), f32), dma((2,))],
        name="arrange",
    )(own, other)


def solution(mesh):
    return jax.shard_map(
        per_device,
        mesh=mesh,
        in_specs=(P("tensor", "context"),) * 3,
        out_specs=(P("tensor", "context"),) * 2,
        check_vma=False,
    )
```

```python
import functools

import jax
import jax.numpy as jnp
import numpy as np
from jax import lax
from jax.experimental import pallas as pl
from jax.experimental.pallas import tpu as pltpu
from jax.sharding import PartitionSpec as P

PLANE = 16
HALF = 4
GROUP = 8
A, B = 64, 128
BLOCK = A * B
Z1_CUT = 3
I_LAG = 3


def split_bf16(table):
    high = table.astype(jnp.bfloat16)
    low = (table - high.astype(np.float64)).astype(jnp.bfloat16)
    return high, low


def tables():
    a, b = np.arange(A), np.arange(B)
    first = 2 * np.pi * (np.arange(A)[:, None] + 0.25) * a[None, :] / A
    last = 2 * np.pi * (np.arange(B)[:, None] * b[None, :] % B) / B
    twist = -2 * np.pi * (np.arange(A)[:, None] + 0.25) * b[None, :] / BLOCK
    fwd1 = np.concatenate([np.cos(first), -np.sin(first)], 0)
    fwd2 = np.block([[np.cos(last), -np.sin(last)], [np.sin(last), np.cos(last)]])
    inv1 = np.block([[np.cos(last), np.sin(last)], [-np.sin(last), np.cos(last)]])
    inv2 = np.concatenate([np.cos(first).T, -np.sin(first).T], 1) / BLOCK
    h, l = split_bf16(fwd1)
    fwd1 = np.concatenate([h, l, h], 1)
    h, l = split_bf16(fwd2)
    fwd2 = np.concatenate([h, l, h], 0)
    h, l = split_bf16(inv1)
    inv1 = np.concatenate([h, l, h], 0)
    h, l = split_bf16(inv2)
    inv2 = np.concatenate([h, l, h], 1)
    turn = np.stack([np.cos(twist), np.sin(twist)]).astype(np.float32)
    return fwd1, fwd2, inv1, inv2, turn


def tripled(value, axis):
    high = value.astype(jnp.bfloat16)
    low = (value - high.astype(jnp.float32)).astype(jnp.bfloat16)
    return jnp.concatenate([high, high, low], axis=axis)


def mm(left, right):
    return jnp.dot(left, right, preferred_element_type=jnp.float32)


def kernel(
    x_hbm, g_hbm, r_hbm, fwd1_hbm, fwd2_hbm, inv1_hbm, inv2_hbm, turn_hbm,
    yout, yrecv,
    raw, rows, mine, vin, fsend, frecv, bsend, brecv, ybuf,
    fwd1, fwd2, inv1, inv2, turn, passing,
    in_sem, z1s, z1r, ps, pr, fs, fr, bs, br, z2s, z2r, ready,
):
    ctx = lax.axis_index("context")
    tens = lax.axis_index("tensor")
    h = ctx & 1
    m = ctx >> 1
    gx, gy = m >> 2, m & 3
    group = (gx + gy) & 1
    place = 2 * gx + (gy >> 1)
    z = 8 * h + (tens >> 1)
    partner = {"context": ctx ^ 1}

    def row_peer(i):
        return {"context": 2 * ((m & 12) + ((m + i) & 3)) + h}

    def along_z(far):
        to = (z + far) & 15
        return {"context": 2 * m + (to >> 3), "tensor": 2 * (to & 7) + (tens & 1)}

    loads = [
        pltpu.make_async_copy(src, dst, in_sem.at[i])
        for i, (src, dst) in enumerate(
            [(x_hbm, raw.at[0]), (g_hbm, raw.at[1]), (r_hbm, raw.at[2]),
             (fwd1_hbm, fwd1), (fwd2_hbm, fwd2), (inv1_hbm, inv1), (inv2_hbm, inv2), (turn_hbm, turn)]
        )
    ]
    for copy in loads[:3]:
        copy.start()
    barrier = pltpu.get_barrier_semaphore()
    pl.semaphore_signal(barrier, 1, device_id=along_z(4))
    pl.semaphore_signal(barrier, 1, device_id=along_z(12))
    for i in range(1, 4):
        pl.semaphore_signal(barrier, 1, device_id={"context": 2 * ((m + 4 * i) & 15) + h})
        pl.semaphore_signal(barrier, 1, device_id=row_peer(i))
    for s in range(3):
        loads[s].wait()
        for a in range(32):
            rows[s, 8 * a : 8 * a + 8, :] = raw[s, :, 128 * a : 128 * a + 128]
        for c in range(HALF):
            mine[c, s] = rows[s, pl.ds(HALF * (1 - h) + c, 32, stride=8), :]

    def way(c, i):
        return 4 + 8 * ((c + i) & 1)

    def z1(c, i):
        return pltpu.make_async_remote_copy(
            mine.at[c, i], passing.at[c, i], z1s.at[c, i], pr.at[c, i], device_id=along_z(way(c, i))
        )

    def z1_on(c, i):
        side = ((z + way(c, i)) & 15) >> 3
        return pltpu.make_async_remote_copy(
            passing.at[c, i], vin.at[c, 1 - side, i], ps.at[c, i], z1r.at[c, i], device_id=along_z(way(c, i))
        )

    def z1_in(c, i):
        return pltpu.make_async_remote_copy(
            passing.at[c, i], vin.at[c, 1 - h, i], ps.at[c, i], z1r.at[c, i], device_id=along_z(way(c, i))
        )

    def z2(c):
        return pltpu.make_async_remote_copy(
            ybuf.at[c, 1 - h], yrecv.at[c], z2s.at[c], z2r.at[c], device_id=partner
        )

    def member(q, side):
        x = q >> 1
        return 4 * x + 2 * (q & 1) + ((side + x) & 1)

    def fwd(c, q):
        return pltpu.make_async_remote_copy(
            fsend.at[c, q], frecv.at[c >> 1, m], fs.at[c], fr.at[c >> 1],
            device_id={"context": 2 * member(q, c & 1) + h},
        )

    def fwd_all(c, count):
        return pltpu.make_async_remote_copy(
            fsend.at[c, pl.ds(0, count)], frecv.at[c >> 1, pl.ds(0, count)], fs.at[c], fr.at[c >> 1], device_id=partner
        )

    def fwd_in(slot):
        part = frecv.at[slot, pl.ds(0, PLANE - 1)]
        return pltpu.make_async_remote_copy(part, part, fs.at[0], fr.at[slot], device_id=partner)

    def back(c, k):
        return pltpu.make_async_remote_copy(
            bsend.at[c >> 1, k], brecv.at[c, place], bs.at[c >> 1], br.at[c], device_id={"context": 2 * k + h}
        )

    def back_in(c, count):
        part = brecv.at[c, pl.ds(0, count)]
        return pltpu.make_async_remote_copy(part, part, bs.at[0], br.at[c], device_id=partner)

    def back_out(slot):
        part = bsend.at[slot, pl.ds(0, PLANE - 1)]
        return pltpu.make_async_remote_copy(part, part, bs.at[slot], br.at[0], device_id=partner)

    pl.semaphore_wait(barrier, 8)

    @pl.loop(0, HALF)
    def _(c):
        for i in range(Z1_CUT):
            z1(c, i).start()

    for i in range(1, 4):
        pl.semaphore_signal(ready, 1, device_id=row_peer(i))
    for copy in loads[3:]:
        copy.start()
    for s in range(3):
        for c in range(HALF):
            vin[c, h, s] = rows[s, pl.ds(HALF * h + c, 32, stride=8), :]
    for copy in loads[3:]:
        copy.wait()

    @pl.loop(0, HALF)
    def _(c):
        for i in range(Z1_CUT):
            z1(c, i).wait_recv()
            z1_on(c, i).start()

    pl.semaphore_wait(ready, 3)

    def forward(c):
        for i in range(Z1_CUT):
            z1_in(c, i).wait_recv()
        value = jnp.concatenate(
            [jnp.concatenate([vin[c, half, s] for half in range(2)], axis=0) for s in range(3)], axis=1
        )
        part = mm(fwd1[...], tripled(value, 0))
        tr, ti = turn[0], turn[1]
        turned = []
        for s in range(3):
            re, im = part[:A, B * s : B * (s + 1)], part[A:, B * s : B * (s + 1)]
            turned.append(jnp.concatenate([re * tr - im * ti, re * ti + im * tr], axis=1))
        spec = mm(tripled(jnp.concatenate(turned, axis=0), 1), fwd2[...])
        for q in range(GROUP):
            for s in range(3):
                fsend[c, q, s] = spec[A * s + 8 * q : A * s + 8 * q + 8, :]

        for i in range(1, GROUP):
            fwd(c, (place + i) & 7).start()

        @pl.when((c & 1) != group)
        def _():
            fwd(c, place).start()

    def middle(c):
        slot = c >> 1
        frecv[slot, m] = fsend[c, place]
        fwd_in(slot).wait_recv()

        def spec(n, s):
            return frecv[slot, n, s, :, :B], frecv[slot, n, s, :, B:]

        folded = []
        for n in range(PLANE):
            re, im = spec(n, 1)
            if n + 1 < PLANE:
                next_re, next_im = spec(n + 1, 1)
                re, im = re + next_im, im - next_re
            folded.append((re, im))
        for k in range(PLANE):
            for out, s in enumerate((2, 0)):
                total_re = total_im = None
                for n in range(PLANE - k):
                    re, im = spec(n, s)
                    wr, wi = folded[n + k]
                    add_re, add_im = re * wr + im * wi, re * wi - im * wr
                    total_re = add_re if total_re is None else total_re + add_re
                    total_im = add_im if total_im is None else total_im + add_im
                bsend[slot, k, out, :, :B] = total_re
                bsend[slot, k, out, :, B:] = total_im

            @pl.when(m != k)
            def _(k=k):
                back(c, k).start()

        brecv[c, place] = bsend[slot, m]

    def inverse(c):
        @pl.when((c & 1) == group)
        def _():
            back_in(c, GROUP - 1).wait_recv()

        @pl.when((c & 1) != group)
        def _():
            back_in(c, GROUP).wait_recv()

        value = jnp.concatenate([brecv[c, q, out] for out in range(2) for q in range(GROUP)], axis=0)
        part = mm(tripled(value, 1), inv1[...])
        tr, ti = turn[0], turn[1]
        turned = []
        for out in range(2):
            re, im = part[A * out : A * (out + 1), :B], part[A * out : A * (out + 1), B:]
            turned.append(jnp.concatenate([re * tr + im * ti, im * tr - re * ti], axis=0))
        y = mm(inv2[...], tripled(jnp.concatenate(turned, axis=1), 0))
        for out in range(2):
            for half in range(2):
                ybuf[c, half, out] = y[32 * half : 32 * (half + 1), B * out : B * (out + 1)]
        z2(c).start()

    @pl.loop(0, HALF)
    def _(c):
        forward(c)

    @pl.loop(0, HALF + I_LAG)
    def _(step):
        @pl.when((step < HALF) & ((step & 1) == group))
        def _():
            middle(step)

        @pl.when(step >= I_LAG)
        def _():
            inverse(step - I_LAG)

    @pl.loop(0, HALF)
    def _(c):
        for i in range(Z1_CUT):
            z1(c, i).wait_send()
            z1_on(c, i).wait_send()

        @pl.when((c & 1) == group)
        def _():
            fwd_all(c, GROUP - 1).wait_send()
            back_out(c >> 1).wait_send()

        @pl.when((c & 1) != group)
        def _():
            fwd_all(c, GROUP).wait_send()

    own = [pltpu.make_async_copy(ybuf.at[c, h], yout.at[c], in_sem.at[c]) for c in range(HALF)]
    for copy in own:
        copy.start()
    for copy in own:
        copy.wait()

    @pl.loop(0, HALF)
    def _(c):
        z2(c).wait()


def arrange(own_hbm, other_hbm, dx_ref, dr_ref, own, other, sem):
    h = lax.axis_index("context") & 1
    copies = [pltpu.make_async_copy(own_hbm, own, sem.at[0]), pltpu.make_async_copy(other_hbm, other, sem.at[1])]
    for copy in copies:
        copy.start()
    for copy in copies:
        copy.wait()
    for out, ref in enumerate((dx_ref, dr_ref)):
        low = [jnp.where(h == 0, own[c, out], other[c, out]) for c in range(HALF)]
        high = [jnp.where(h == 0, other[c, out], own[c, out]) for c in range(HALF)]
        turned = jnp.stack(low + high, axis=1)
        for a in range(32):
            ref[:, 128 * a : 128 * a + 128] = turned[a]


def per_device(inputs, grads, response):
    consts = tables()
    f32, bf16 = jnp.float32, jnp.bfloat16
    vmem, dma = pltpu.VMEM, pltpu.SemaphoreType.DMA
    own, other = pl.pallas_call(
        kernel,
        out_shape=(jax.ShapeDtypeStruct((HALF, 2, 32, B), f32),) * 2,
        in_specs=[pl.BlockSpec(memory_space=pl.ANY)] * 8,
        out_specs=(pl.BlockSpec(memory_space=pl.ANY),) * 2,
        scratch_shapes=[
            vmem((3, 8, 4096), f32),
            vmem((3, 256, 128), f32),
            vmem((HALF, Z1_CUT, 32, 128), f32),
            vmem((HALF, 2, Z1_CUT, 32, 128), f32),
            vmem((HALF, GROUP, 3, 8, 2 * B), f32),
            vmem((2, PLANE, 3, 8, 2 * B), f32),
            vmem((2, PLANE, 2, 8, 2 * B), f32),
            vmem((HALF, GROUP, 2, 8, 2 * B), f32),
            vmem((HALF, 2, 2, 32, 128), f32),
            vmem((2 * A, 3 * A), bf16),
            vmem((6 * B, 2 * B), bf16),
            vmem((6 * B, 2 * B), bf16),
            vmem((A, 6 * A), bf16),
            vmem((2, A, B), f32),
            vmem((HALF, Z1_CUT, 32, B), f32),
            dma((8,)),
            dma((HALF, Z1_CUT)), dma((HALF, Z1_CUT)),
            dma((HALF, Z1_CUT)), dma((HALF, Z1_CUT)),
            dma((HALF,)), dma((2,)),
            dma((2,)), dma((HALF,)),
            dma((HALF,)), dma((HALF,)),
            pltpu.SemaphoreType.REGULAR,
        ],
        compiler_params=pltpu.CompilerParams(collective_id=0, has_side_effects=True),
        name="hyena_backward",
    )(inputs, grads, response, *(jnp.asarray(t) for t in consts))
    return pl.pallas_call(
        arrange,
        out_shape=(jax.ShapeDtypeStruct(inputs.shape, f32),) * 2,
        in_specs=[pl.BlockSpec(memory_space=pl.ANY)] * 2,
        out_specs=(pl.BlockSpec(memory_space=vmem),) * 2,
        scratch_shapes=[vmem((HALF, 2, 32, B), f32), vmem((HALF, 2, 32, B), f32), dma((2,))],
        name="arrange",
    )(own, other)


def solution(mesh):
    return jax.shard_map(
        per_device,
        mesh=mesh,
        in_specs=(P("tensor", "context"),) * 3,
        out_specs=(P("tensor", "context"),) * 2,
        check_vma=False,
    )
```
